32 devices in a mesh: tm: 8 (over z, y), row: 4 (over x, core).
Axes of the slice: x: 2, y: 2, z: 4, core: 2. Of those that a mesh axis runs over, the one named last changes fastest.
Arguments:
- lower: bfloat16 [16, 1024, 1024], P('tm', 'row'), may hold values from -0.1875 to 0.1875
- upper: bfloat16 [16, 1024, 1024], P('tm', 'row'), may hold values from -0.1875 to 0.1875
- shift_diag: float32 [16, 1024], P('tm', 'row'), may hold values from -0.5 to 0.5
- rhs: float32 [16, 1024, 128], P('tm', 'row'), may hold values from -6 to 6
Outputs:
- lower_two: bfloat16 [16, 1024, 1024], P('tm', 'row')
- upper_two: bfloat16 [16, 1024, 1024], P('tm', 'row')
- excess_two: bfloat16 [16, 1024, 1024], P('tm', 'row')
- rhs_two: float32 [16, 1024, 128], P('tm', 'row')
The draws below stay inside these ranges and needn't reach their ends.
All inputs are finite; a program needn't handle non-finite values.
Results may differ from the reference program's by a relative error of at most 0.0083.
Values may be sent and summed in bfloat16 or wider, within the bound.
No kernel may reach another device: no remote copies, remote signals or barrier semaphores. Data moves between devices by JAX's collectives and lax.ppermute only.
A program may use at most 128 MiB of HBM per device.

```python
import jax
import jax.numpy as jnp

NS = 1024
RHS = 128
NT = 16


def levels(rng, extent, split, smallest, largest):
    def one(dim, blocks):
        heights = jax.random.uniform(jax.random.fold_in(jax.random.fold_in(rng, 6), dim), (blocks,), jnp.float32, smallest / len(split), largest / len(split))
        return jnp.repeat(jnp.exp(heights), extent[dim] // blocks).reshape((-1,) + (1,) * (len(extent) - dim - 1))

    loudness = one(*split[0])
    for cut in split[1:]:
        loudness = loudness * one(*cut)
    return loudness


def scatter_about(rng, extent, deviation, limit, shards=(), kind=jnp.bfloat16):
    array = jax.random.normal(rng, extent, jnp.float32) * deviation
    if len(shards) > 0:
        array = levels(rng, extent, shards, -0.22, 0.18) * array
    return jnp.clip(array, min=-limit, max=limit).astype(kind)


def setup_inputs(seed: int = 0) -> dict:
    key_of = jax.random.split(jax.random.key(seed), 5)
    lower = scatter_about(key_of[0], (NT, NS, NS), NS ** -0.5, 0.1875, ((0, 8), (1, 4)))
    upper = scatter_about(key_of[1], (NT, NS, NS), NS ** -0.5, 0.1875, ((0, 8), (1, 4)))
    shift_diag = jnp.clip(jax.random.uniform(key_of[2], (NT, NS), jnp.float32, -0.5, 0.5) * levels(key_of[2], (NT, NS), ((0, 8), (1, 4)), -0.4, 0.0), -0.5, 0.5)
    rhs = scatter_about(key_of[3], (NT, NS, RHS), 1.0, 6.0, ((0, 8), (1, 4)), jnp.float32)
    return dict(lower=lower, upper=upper, shift_diag=shift_diag, rhs=rhs)


def shift_sections(values, distance):
    filler = jnp.zeros((abs(distance),) + values.shape[1:], values.dtype)
    if distance > 0:
        return jnp.concatenate([filler, values[:-distance]], axis=0)
    return jnp.concatenate([values[-distance:], filler], axis=0)


def batched(left_blocks, right_blocks):
    return jnp.einsum("tij,tjk->tik", left_blocks.astype(jnp.float32), right_blocks.astype(jnp.float32))


def level_terms(lower_blocks, upper_blocks, panel, distance):
    below_term = batched(lower_blocks, shift_sections(panel, distance))
    above_term = batched(upper_blocks, shift_sections(panel, -distance))
    return below_term, above_term


def reference(lower, upper, shift_diag, rhs):
    states = lower.shape[1]
    scaling = 1.0 - shift_diag
    panel_one = (scaling[:, :, None] * jnp.concatenate([lower.astype(jnp.float32), upper.astype(jnp.float32), rhs], axis=2)).astype(jnp.bfloat16)
    below_one, above_one = level_terms(lower, upper, panel_one, 1)
    identity = jnp.eye(states, dtype=jnp.float32)
    lower_one = (-below_one[:, :, :states]).astype(jnp.bfloat16)
    upper_one = (-above_one[:, :, states:2 * states]).astype(jnp.bfloat16)
    excess_one = (shift_diag[:, :, None] * identity[None] - below_one[:, :, states:2 * states] - above_one[:, :, :states]).astype(jnp.bfloat16)
    rhs_one = rhs - below_one[:, :, 2 * states:] - above_one[:, :, 2 * states:]
    own_blocks = jnp.concatenate([lower_one, upper_one, rhs_one.astype(jnp.bfloat16)], axis=2)
    panel_two = (own_blocks.astype(jnp.float32) - batched(excess_one, own_blocks)).astype(jnp.bfloat16)
    below_two, above_two = level_terms(lower_one, upper_one, panel_two, 2)
    lower_two = (-below_two[:, :, :states]).astype(jnp.bfloat16)
    upper_two = (-above_two[:, :, states:2 * states]).astype(jnp.bfloat16)
    excess_two = (excess_one.astype(jnp.float32) - below_two[:, :, states:2 * states] - above_two[:, :, :states]).astype(jnp.bfloat16)
    rhs_two = rhs_one - below_two[:, :, 2 * states:] - above_two[:, :, 2 * states:]
    return lower_two, upper_two, excess_two, rhs_two
```

```python
import jax
import jax.numpy as jnp
from jax import lax
from jax.sharding import PartitionSpec as P

AXES = ("tm", "row")


def from_behind(array, axis, by):
    count = lax.axis_size(axis)
    pairs = [(i, i + by) for i in range(count) if 0 <= i + by < count]
    return lax.ppermute(array, axis, pairs)


def stacked(left_blocks, right_blocks):
    return jnp.einsum("bij,bjk->bik", left_blocks, right_blocks, preferred_element_type=jnp.float32)


def neighbour_terms(lower_rows, upper_rows, panel_rows, distance):
    below_in = from_behind(panel_rows[-distance:], "tm", 1)
    above_in = from_behind(panel_rows[:distance], "tm", -1)
    below_panel = jnp.concatenate([below_in, panel_rows[:-distance]], axis=0)
    above_panel = jnp.concatenate([panel_rows[distance:], above_in], axis=0)
    below_full = lax.all_gather(below_panel, "row", axis=1, tiled=True)
    above_full = lax.all_gather(above_panel, "row", axis=1, tiled=True)
    return (stacked(lower_rows, below_full), stacked(upper_rows, above_full))


def apply_terms(below_term, above_term, excess_rows, rhs_rows, states):
    lower_new = (-below_term[:, :, :states]).astype(jnp.bfloat16)
    upper_new = (-above_term[:, :, states : 2 * states]).astype(jnp.bfloat16)
    excess_new = (
        excess_rows - below_term[:, :, states : 2 * states] - above_term[:, :, :states]
    ).astype(jnp.bfloat16)
    rhs_new = rhs_rows - below_term[:, :, 2 * states :] - above_term[:, :, 2 * states :]
    return (lower_new, upper_new, excess_new, rhs_new)


def shards_by_rows(lower, upper, shift_diag, rhs):
    groups, height, states = lower.shape
    offset = lax.axis_index("row") * height
    columns = lax.broadcasted_iota(jnp.int32, (groups, height, states), 2)
    row_pos = lax.broadcasted_iota(jnp.int32, (groups, height, states), 1) + offset
    excess_zero = jnp.where(columns == row_pos, shift_diag[:, :, None], 0.0)
    panel_one = scaled_panel(lower, upper, shift_diag, rhs)
    below_one, above_one = neighbour_terms(lower, upper, panel_one, 1)
    lower_one, upper_one, excess_one, rhs_one = apply_terms(
        below_one, above_one, excess_zero, rhs, states
    )
    own_rows = jnp.concatenate([lower_one, upper_one, rhs_one.astype(jnp.bfloat16)], axis=2)
    product = stacked(excess_one, lax.all_gather(own_rows, "row", axis=1, tiled=True))
    panel_two = (own_rows.astype(jnp.float32) - product).astype(jnp.bfloat16)
    below_two, above_two = neighbour_terms(lower_one, upper_one, panel_two, 2)
    return apply_terms(below_two, above_two, excess_one.astype(jnp.float32), rhs_one, states)


def scaled_panel(lower, upper, shift_diag, rhs):
    scaling = (1.0 - shift_diag)[..., None]
    parts = [lower.astype(jnp.float32), upper.astype(jnp.float32), rhs]
    return (scaling * jnp.concatenate(parts, axis=-1)).astype(jnp.bfloat16)


def dot(left, right):
    return jnp.dot(left, right, preferred_element_type=jnp.float32)


def shards_by_blocks(lower, upper, shift_diag, rhs):
    height, states = lower.shape[1:]
    scenarios = rhs.shape[2]
    half = states // 2
    planes = lax.axis_size("tm") // 2
    group, row = lax.axis_index("tm"), lax.axis_index("row")
    y, z, x, k = group % 2, group // 2, row // 2, row % 2
    home = k == y

    def send(array, to):
        pairs = []
        for device in range(planes * 8):
            gz, gy, gx, gk = device // 8, device // 4 % 2, device // 2 % 2, device % 2
            target = to(gx, gy, gz, gk)
            if target is not None and 0 <= target[2] < planes:
                tx, ty, tz, tk = target
                pairs.append((device, tz * 8 + ty * 4 + tx * 2 + tk))
        return lax.ppermute(array, AXES, pairs)

    def swap(array):
        return send(array, lambda x, y, z, k: (x, y, z, 1 - k))

    def across_x(array):
        return send(array, lambda x, y, z, k: (1 - x, y, z, k))

    def to_away(array):
        first = send(array, lambda x, y, z, k: (x, 1 - y, z, y) if k == y else None)
        second = send(array, lambda x, y, z, k: (x, 1 - y, z, y) if k != y else None)
        return first, second

    def away_x(array):
        return send(array, lambda x, y, z, k: (1 - x, y, z, k) if k != y else None)

    def away_to_home_z(array):
        return send(array, lambda x, y, z, k: (x, y, z + 1 - 2 * y, y) if k != y else None)

    quarters = scaled_panel(lower, upper, shift_diag, rhs)
    outer = lax.dynamic_index_in_dim(quarters, y, 0, False)
    inner = lax.dynamic_index_in_dim(quarters, 1 - y, 0, False)
    shifts = lax.all_gather(shift_diag, AXES, axis=0, tiled=False)

    far_a, far_b = to_away(outer)
    inner_x = across_x(inner)
    inner_k = swap(inner)
    outer_k = send(outer, lambda x, y, z, k: (x, y, z, y) if k != y else None)
    centre_a, centre_b = to_away(inner)
    far_xa, far_xb = away_x(far_a), away_x(far_b)
    halo_a, halo_b = away_to_home_z(far_b), away_to_home_z(far_a)
    outer_late, _ = lax.optimization_barrier((outer, (far_a, far_b)))
    outer_xa = send(outer_late, lambda x, y, z, k: (1 - x, y, z, y) if k == y else None)
    outer_xb = send(outer_late, lambda x, y, z, k: (1 - x, y, z, y) if k != y else None)
    inner_xk = swap(inner_x)
    centre_xa, centre_xb = to_away(inner_x)
    halo_xa, halo_xb = away_to_home_z(far_xb), away_to_home_z(far_xa)

    def assembled(own_a, own_b, other_a, other_b):
        panel = jnp.zeros((states, 2 * states + scenarios), jnp.bfloat16)
        for piece, px, pk in (
            (own_a, x, k), (own_b, x, 1 - k), (other_a, 1 - x, k), (other_b, 1 - x, 1 - k)
        ):
            panel = lax.dynamic_update_slice_in_dim(panel, piece, px * half + pk * height, 0)
        return panel

    def pick(at_home, away):
        return jnp.where(home, at_home, away)

    near = assembled(inner, inner_k, inner_x, inner_xk)
    far = assembled(
        pick(halo_a, far_a), pick(halo_b, far_b), pick(halo_xa, far_xa), pick(halo_xb, far_xb)
    )
    centre = assembled(
        pick(outer, centre_a), pick(outer_k, centre_b),
        pick(outer_xa, centre_xa), pick(outer_xb, centre_xb),
    )

    near_at, far_at = (1 - k) * states, k * states

    def columns(array, at, width=states):
        return lax.dynamic_slice_in_dim(array, at, width, 1)

    shift = lax.dynamic_slice_in_dim(shifts, (2 * z + k) * 4, 4, 0)
    shift = lax.dynamic_index_in_dim(shift, y, 1, False).reshape(states, 1)
    unscale = 1.0 / (1.0 - shift)
    near_term = unscale * dot(columns(centre, near_at), near)
    far_term = unscale * dot(columns(centre, far_at), far)
    near_one = (-columns(near_term, near_at)).astype(jnp.bfloat16)
    far_one = (-columns(far_term, far_at)).astype(jnp.bfloat16)
    diagonal = jnp.where(
        lax.broadcasted_iota(jnp.int32, (states, states), 0)
        == lax.broadcasted_iota(jnp.int32, (states, states), 1),
        shift, 0.0,
    )
    excess_one = (diagonal - columns(near_term, far_at) - columns(far_term, near_at)).astype(
        jnp.bfloat16
    )
    rhs_one = (
        unscale * centre[:, 2 * states :].astype(jnp.float32)
        - near_term[:, 2 * states :]
        - far_term[:, 2 * states :]
    )

    own = jnp.concatenate(
        [columns(near_one, x * half, half), columns(far_one, x * half, half),
         rhs_one.astype(jnp.bfloat16)], axis=1,
    )
    panel_two = (own.astype(jnp.float32) - dot(excess_one, own)).astype(jnp.bfloat16)
    near_two = swap(panel_two)
    far_two = send(panel_two, lambda x, y, z, k: (x, y, z - 1 + 2 * k, 1 - k))
    near_out = dot(near_one, near_two)
    far_out = dot(far_one, far_two)
    near_new = (-near_out[:, half:states]).astype(jnp.bfloat16)
    far_new = (-far_out[:, :half]).astype(jnp.bfloat16)
    excess_new = (
        columns(excess_one, x * half, half).astype(jnp.float32)
        - near_out[:, :half]
        - far_out[:, half:states]
    ).astype(jnp.bfloat16)
    rhs_new = rhs_one - near_out[:, states:] - far_out[:, states:]

    def at_home(array, width, crosses=(0, 1)):
        placed = jnp.zeros((2, height, width), array.dtype)
        for other_x in crosses:
            for flip in (0, 1):
                at = (x ^ other_x) * half + (y ^ flip) * height
                piece = lax.dynamic_slice_in_dim(array, at, height, 0)
                piece = send(piece, lambda x, y, z, k: (x ^ other_x, k, z, y ^ flip))
                start = (k ^ flip, 0, (x ^ other_x) * half if len(crosses) > 1 else 0)
                placed = lax.dynamic_update_slice(placed, piece[None], start)
        return placed

    near_home, far_home, excess_home = (
        at_home(part, states) for part in (near_new, far_new, excess_new)
    )
    rhs_home = at_home(rhs_new, scenarios, (0,))
    lower_two = jnp.where(y == 0, far_home, near_home)
    upper_two = jnp.where(y == 0, near_home, far_home)
    return lower_two, upper_two, excess_home, rhs_home


def solution(mesh):
    paired = mesh.shape["row"] == 4 and mesh.shape["tm"] % 2 == 0
    spec = P("tm", "row", None)

    def program(lower, upper, shift_diag, rhs):
        two_blocks = lower.shape[0] == 2 * mesh.shape["tm"]
        return jax.shard_map(
            shards_by_blocks if paired and two_blocks else shards_by_rows,
            mesh=mesh,
            in_specs=(spec, spec, P("tm", "row"), spec),
            out_specs=(spec,) * 4,
            check_vma=False,
        )(lower, upper, shift_diag, rhs)

    return program
```

```python
import jax
import jax.numpy as jnp
from jax import lax
from jax.experimental import pallas as pl
from jax.experimental.pallas import tpu as pltpu
from jax.sharding import PartitionSpec as P

AXES = ("tm", "row")
LANES = 128


def from_behind(array, axis, by):
    count = lax.axis_size(axis)
    pairs = [(i, i + by) for i in range(count) if 0 <= i + by < count]
    return lax.ppermute(array, axis, pairs)


def stacked(left_blocks, right_blocks):
    return jnp.einsum("bij,bjk->bik", left_blocks, right_blocks, preferred_element_type=jnp.float32)


def neighbour_terms(lower_rows, upper_rows, panel_rows, distance):
    below_in = from_behind(panel_rows[-distance:], "tm", 1)
    above_in = from_behind(panel_rows[:distance], "tm", -1)
    below_panel = jnp.concatenate([below_in, panel_rows[:-distance]], axis=0)
    above_panel = jnp.concatenate([panel_rows[distance:], above_in], axis=0)
    below_full = lax.all_gather(below_panel, "row", axis=1, tiled=True)
    above_full = lax.all_gather(above_panel, "row", axis=1, tiled=True)
    return (stacked(lower_rows, below_full), stacked(upper_rows, above_full))


def apply_terms(below_term, above_term, excess_rows, rhs_rows, states):
    lower_new = (-below_term[:, :, :states]).astype(jnp.bfloat16)
    upper_new = (-above_term[:, :, states : 2 * states]).astype(jnp.bfloat16)
    excess_new = (
        excess_rows - below_term[:, :, states : 2 * states] - above_term[:, :, :states]
    ).astype(jnp.bfloat16)
    rhs_new = rhs_rows - below_term[:, :, 2 * states :] - above_term[:, :, 2 * states :]
    return (lower_new, upper_new, excess_new, rhs_new)


def shards_by_rows(lower, upper, shift_diag, rhs):
    groups, height, states = lower.shape
    offset = lax.axis_index("row") * height
    columns = lax.broadcasted_iota(jnp.int32, (groups, height, states), 2)
    row_pos = lax.broadcasted_iota(jnp.int32, (groups, height, states), 1) + offset
    excess_zero = jnp.where(columns == row_pos, shift_diag[:, :, None], 0.0)
    panel_one = scaled_panel(lower, upper, shift_diag, rhs)
    below_one, above_one = neighbour_terms(lower, upper, panel_one, 1)
    lower_one, upper_one, excess_one, rhs_one = apply_terms(
        below_one, above_one, excess_zero, rhs, states
    )
    own_rows = jnp.concatenate([lower_one, upper_one, rhs_one.astype(jnp.bfloat16)], axis=2)
    product = stacked(excess_one, lax.all_gather(own_rows, "row", axis=1, tiled=True))
    panel_two = (own_rows.astype(jnp.float32) - product).astype(jnp.bfloat16)
    below_two, above_two = neighbour_terms(lower_one, upper_one, panel_two, 2)
    return apply_terms(below_two, above_two, excess_one.astype(jnp.float32), rhs_one, states)


def scaled_panel(lower, upper, shift_diag, rhs):
    scaling = (1.0 - shift_diag)[..., None]
    parts = [lower.astype(jnp.float32), upper.astype(jnp.float32), rhs]
    return (scaling * jnp.concatenate(parts, axis=-1)).astype(jnp.bfloat16)


def dot(left, right):
    return jnp.dot(left, right, preferred_element_type=jnp.float32)


def call(kernel, outs, *arrays, scratch=(), **grid):
    if not grid:
        grid = dict(
            in_specs=[whole(array.shape) for array in arrays[1:]],
            out_specs=[whole(out.shape) for out in outs],
            grid=(1,),
        )
    return pl.pallas_call(
        kernel,
        out_shape=outs,
        grid_spec=pltpu.PrefetchScalarGridSpec(
            num_scalar_prefetch=1, scratch_shapes=list(scratch), **grid
        ),
        compiler_params=pltpu.CompilerParams(vmem_limit_bytes=32 << 20),
    )(*arrays)


def whole(shape):
    return pl.BlockSpec(shape, lambda *_: (0,) * len(shape))


def shaped(shape, dtype=jnp.bfloat16):
    return jax.ShapeDtypeStruct(shape, dtype)


def pack(place, lower, upper, shift_diag, rhs):
    height, states = lower.shape[1:]
    scenarios = rhs.shape[2]
    width = 2 * states + scenarios
    rows = height // 2

    def kernel(place_ref, lower_ref, upper_ref, shift_ref, rhs_ref, outer, inner_all, first, second):
        y, home = place_ref[1], place_ref[4]
        across = lax.broadcasted_iota(jnp.int32, (rows, height), 1)
        down = lax.broadcasted_iota(jnp.int32, (rows, height), 0) + pl.program_id(0) * rows

        lane = lax.broadcasted_iota(jnp.int32, (rows, LANES), 1)

        def panel(block, *outs):
            shift = jnp.broadcast_to(shift_ref[pl.ds(block, 1), :], (rows, height))
            shift = jnp.sum(jnp.where(across == down, shift, 0.0), axis=1, keepdims=True)
            for at, ref in ((0, lower_ref), (states, upper_ref), (2 * states, rhs_ref)):
                part = ((1.0 - shift) * ref[block].astype(jnp.float32)).astype(jnp.bfloat16)
                for out in outs:
                    if out is not None:
                        out[:, at : at + part.shape[1]] = part
            tail = jnp.zeros((rows, LANES), jnp.float32)
            for index in range(3):
                part = shift.astype(jnp.bfloat16).astype(jnp.float32)
                tail = jnp.where(lane == index, part, tail)
                shift = shift - part
            for out in outs[1:]:
                out[:, width:] = tail.astype(jnp.bfloat16)

        @pl.when(home == 1)
        def _():
            panel(y, outer, second)
            panel(1 - y, None, inner_all, first)

        @pl.when(home == 0)
        def _():
            panel(y, outer, first)
            panel(1 - y, None, inner_all, second)

    def rows_of(array):
        return pl.BlockSpec((2, rows, array.shape[2]), lambda i, _: (0, i, 0))

    return call(
        kernel,
        [shaped((height, width))] + [shaped((height, width + LANES))] * 3,
        place, lower, upper, shift_diag, rhs,
        grid=(2,),
        in_specs=[rows_of(lower), rows_of(upper), whole(shift_diag.shape), rows_of(rhs)],
        out_specs=[pl.BlockSpec((rows, width), lambda i, _: (i, 0))]
        + [pl.BlockSpec((rows, width + LANES), lambda i, _: (i, 0))] * 3,
    )


def level_one(place, centre, near, far, scenarios):
    states = centre.shape[0]
    half, tile, chunk = states // 2, states // 4, states // 2
    steps = states // tile

    def kernel(
        place_ref, centre_ref, near_n, near_f, near_r, far_n, far_f, far_r,
        near_out, far_out, excess_out, rhs_out, panel_near, panel_rest, ones, excess_all,
    ):
        step = pl.program_id(0)
        k, x = place_ref[3], place_ref[2]
        near_at = pl.multiple_of((1 - k) * states, states)
        far_at = pl.multiple_of(k * states, states)
        here = pl.ds(pl.multiple_of(step * tile, tile), tile)
        for at in range(0, states, chunk):
            rows = slice(at, at + chunk)
            left_near = centre_ref[rows, pl.ds(near_at, states)]
            left_far = centre_ref[rows, pl.ds(far_at, states)]
            parts = centre_ref[rows, 2 * states + scenarios :].astype(jnp.float32)
            shift_rows = parts[:, 0:1] + parts[:, 1:2] + parts[:, 2:3]
            unscale = 1.0 / (1.0 - shift_rows)
            near_one = (-unscale * dot(left_near, near_n[...])).astype(jnp.bfloat16)
            near_out[rows, :] = near_one
            ones[0, rows, here] = near_one
            far_one = (-unscale * dot(left_far, far_f[...])).astype(jnp.bfloat16)
            far_out[rows, :] = far_one
            ones[1, rows, here] = far_one
            across = lax.broadcasted_iota(jnp.int32, (chunk, tile), 1) + step * tile
            down = lax.broadcasted_iota(jnp.int32, (chunk, tile), 0) + at
            cross = dot(left_near, near_f[...]) + dot(left_far, far_n[...])
            excess = jnp.where(across == down, shift_rows, 0.0) - unscale * cross
            excess = excess.astype(jnp.bfloat16)
            excess_out[rows, :] = excess
            excess_all[rows, here] = excess

            @pl.when(step == 0)
            def _():
                own = centre_ref[rows, 2 * states : 2 * states + scenarios].astype(jnp.float32)
                cross = dot(left_near, near_r[...]) + dot(left_far, far_r[...])
                rhs_out[rows, :] = unscale * (own - cross)

        @pl.when(step == steps - 1)
        def _():
            columns = pl.ds(pl.multiple_of(x * half, half), half)
            rhs_all = rhs_out[...].astype(jnp.bfloat16)
            for at in range(0, states, chunk):
                rows = slice(at, at + chunk)
                excess = excess_all[rows, :]

                def panel(own_all, own):
                    return (own.astype(jnp.float32) - dot(excess, own_all)).astype(jnp.bfloat16)

                panel_near[rows, :] = panel(ones[0, :, columns], ones[0, rows, columns])
                panel_rest[rows, :half] = panel(ones[1, :, columns], ones[1, rows, columns])
                panel_rest[rows, half:] = panel(rhs_all, rhs_all[rows, :])

    def side(flipped):
        def at(step, place_ref):
            k = place_ref[3]
            return (0, (k if flipped else 1 - k) * steps + step)

        return pl.BlockSpec((states, tile), at)

    rest = pl.BlockSpec((states, scenarios), lambda *_: (0, 2 * states // scenarios))
    blocks = pl.BlockSpec((states, tile), lambda step, _: (0, step))
    square = shaped((states, states))
    outs = [square, square, square, shaped((states, scenarios), jnp.float32),
            shaped((states, half)), shaped((states, half + scenarios))]
    return call(
        kernel,
        outs,
        place, centre, near, near, near, far, far, far,
        scratch=[pltpu.VMEM((2, states, states), jnp.bfloat16),
                 pltpu.VMEM((states, states), jnp.bfloat16)],
        grid=(steps,),
        in_specs=[pl.BlockSpec(centre.shape, lambda *_: (0, 0), pipeline_mode=pl.Buffered(1)),
                  side(False), side(True), rest, side(False), side(True), rest],
        out_specs=[blocks] * 3 + [whole(out.shape) for out in outs[3:]],
    )


def message_rows(place_ref, states, message):
    quarter = states // 4
    at = (place_ref[2] ^ (message // 2)) * 2 + (place_ref[1] ^ (message % 2))
    return pl.ds(pl.multiple_of(at * quarter, quarter), quarter)


def messages(place, left, right, width):
    states = left.shape[0]

    def kernel(place_ref, left_ref, right_ref, *outs):
        for message, out in enumerate(outs):
            rows = message_rows(place_ref, states, message)
            out[...] = (-dot(left_ref[rows, :], right_ref[...])).astype(jnp.bfloat16)

    outs = [shaped((states // 4, width))] * 4
    return call(
        kernel, outs, place, left, right,
        grid=(1,),
        in_specs=[whole(left.shape), pl.BlockSpec((states, width), lambda *_: (0, 0))],
        out_specs=[whole(out.shape) for out in outs],
    )


def near_rest(place, left, near, rest, excess, rhs):
    states, half = near.shape
    scenarios = rhs.shape[1]

    def kernel(place_ref, left_ref, near_ref, rest_ref, excess_ref, rhs_ref, excess_out, rhs_out):
        excess_out[...] = excess_ref[...].astype(jnp.float32) - dot(left_ref[...], near_ref[...])
        rhs_out[...] = rhs_ref[...] - dot(left_ref[...], rest_ref[...])

    rows = states // 4

    def by_rows(width, at=lambda place_ref: 0):
        return pl.BlockSpec((rows, width), lambda i, place_ref: (i, at(place_ref)))

    return call(
        kernel,
        [shaped((states, half), jnp.float32), shaped((states, scenarios), jnp.float32)],
        place, left, near, rest, excess, rhs,
        grid=(4,),
        in_specs=[by_rows(states), whole(near.shape),
                  pl.BlockSpec((states, scenarios), lambda *_: (0, half // scenarios)),
                  by_rows(half, lambda place_ref: place_ref[2]), by_rows(scenarios)],
        out_specs=[by_rows(half), by_rows(scenarios)],
    )


def far_rest(place, left, rest, excess, rhs):
    states, half = excess.shape
    scenarios = rhs.shape[1]

    def kernel(place_ref, left_ref, rest_ref, excess_ref, rhs_ref, *outs):
        for message in range(4):
            rows = message_rows(place_ref, states, message)
            product = dot(left_ref[rows, :], rest_ref[:, :half])
            outs[message][...] = (excess_ref[rows, :] - product).astype(jnp.bfloat16)
            if message < 2:
                product = dot(left_ref[rows, :], rest_ref[:, half:])
                outs[4 + message][...] = rhs_ref[rows, :] - product

    quarter = states // 4
    outs = [shaped((quarter, half))] * 4 + [shaped((quarter, scenarios), jnp.float32)] * 2
    return call(kernel, outs, place, left, rest, excess, rhs)


def after(array, *others):
    return lax.optimization_barrier((array, others))[0]


def shards_by_blocks(lower, upper, shift_diag, rhs):
    height, states = lower.shape[1:]
    scenarios = rhs.shape[2]
    half = states // 2
    planes = lax.axis_size("tm") // 2
    group, row = lax.axis_index("tm"), lax.axis_index("row")
    y, z, x, k = group % 2, group // 2, row // 2, row % 2
    home = k == y
    place = jnp.stack([z, y, x, k, home.astype(jnp.int32)])

    def send(array, to):
        pairs = []
        for device in range(planes * 8):
            gz, gy, gx, gk = device // 8, device // 4 % 2, device // 2 % 2, device % 2
            target = to(gx, gy, gz, gk)
            if target is not None and 0 <= target[2] < planes:
                tx, ty, tz, tk = target
                pairs.append((device, tz * 8 + ty * 4 + tx * 2 + tk))
        return lax.ppermute(array, AXES, pairs)

    def swap(array):
        return send(array, lambda x, y, z, k: (x, y, z, 1 - k))

    def across_x(array):
        return send(array, lambda x, y, z, k: (1 - x, y, z, k))

    def away_x(array):
        return send(array, lambda x, y, z, k: (1 - x, y, z, k) if k != y else None)

    def away_to_home_z(array):
        return send(array, lambda x, y, z, k: (x, y, z + 1 - 2 * y, y) if k != y else None)

    outer, inner, first, second = pack(place, lower, upper, shift_diag, rhs)

    far_a = send(outer, lambda x, y, z, k: (x, 1 - y, z, y) if k == y else None)
    far_b = send(outer, lambda x, y, z, k: (x, 1 - y, z, y) if k != y else None)
    inner_x = across_x(inner)
    inner_k = swap(inner)
    centre_a = send(
        after(first, far_a), lambda x, y, z, k: (x, 1 - y, z, y) if k == y else (x, y, z, y)
    )
    far_xa, halo_b = away_x(far_a), away_to_home_z(far_a)
    centre_b = send(
        after(second, far_b), lambda x, y, z, k: (x, y, z, y) if k == y else (x, 1 - y, z, y)
    )
    far_xb, halo_a = away_x(far_b), away_to_home_z(far_b)
    inner_xk = swap(inner_x)
    first_x = after(jnp.where(home, second, inner_x), centre_a, far_xa)
    second_x = after(jnp.where(home, inner_x, first), centre_b, far_xb)
    centre_xa = send(
        first_x, lambda x, y, z, k: (1 - x, y, z, y) if k == y else (x, 1 - y, z, y)
    )
    halo_xb = away_to_home_z(far_xa)
    centre_xb = send(
        second_x, lambda x, y, z, k: (x, 1 - y, z, y) if k == y else (1 - x, y, z, y)
    )
    halo_xa = away_to_home_z(far_xb)

    def assembled(*pieces):
        panel = jnp.zeros((states, pieces[0][0].shape[1]), jnp.bfloat16)
        for piece, px, pk in pieces:
            panel = lax.dynamic_update_slice_in_dim(panel, piece, px * half + pk * height, 0)
        return panel

    def pick(at_home, away):
        return jnp.where(home, at_home, away)

    near = assembled(
        (inner, x, k), (inner_k, x, 1 - k), (inner_x, 1 - x, k), (inner_xk, 1 - x, 1 - k)
    )
    far = assembled(
        (pick(halo_a, far_a), x, k), (pick(halo_b, far_b), x, 1 - k),
        (pick(halo_xa, far_xa), 1 - x, k), (pick(halo_xb, far_xb), 1 - x, 1 - k),
    )
    centre = assembled(
        (centre_b, x, y), (centre_a, x, 1 - y), (centre_xa, 1 - x, y), (centre_xb, 1 - x, 1 - y)
    )

    near_one, far_one, excess_one, rhs_one, panel_near, panel_rest = level_one(
        place, centre, near, far, scenarios
    )

    def across_z(array):
        return send(array, lambda x, y, z, k: (x, y, z - 1 + 2 * k, 1 - k))

    def at_home(pieces):
        return [
            (send(piece, lambda x, y, z, k, m=m: (x ^ (m // 2), k, z, y ^ (m % 2))), m)
            for m, piece in enumerate(pieces)
        ]

    far_two_near = across_z(panel_near)
    near_two_rest = swap(panel_rest)
    near_new = messages(place, near_one, near_two_rest, half)
    near_two_near = swap(panel_near)
    far_two_rest = across_z(after(panel_rest, near_two_rest))
    near_home = at_home(near_new)
    excess_part, rhs_part = near_rest(
        place, near_one, near_two_near, near_two_rest, excess_one, rhs_one
    )
    far_two_near = after(far_two_near, near_new, excess_part)
    far_home = at_home(messages(place, far_one, far_two_near, half))
    last = far_rest(place, far_one, far_two_rest, excess_part, rhs_part)
    excess_home = at_home(last[:4])
    rhs_home = at_home(last[4:])

    def placed(pieces, width, dtype):
        result = jnp.zeros((2, height, width), dtype)
        for piece, m in pieces:
            start = (k ^ (m % 2), 0, (x ^ (m // 2)) * half if len(pieces) > 2 else 0)
            result = lax.dynamic_update_slice(result, piece[None], start)
        return result

    def chosen(ours, theirs):
        return [(jnp.where(y == 0, a, b), m) for (a, m), (b, _) in zip(ours, theirs)]

    lower_two = placed(chosen(far_home, near_home), states, jnp.bfloat16)
    upper_two = placed(chosen(near_home, far_home), states, jnp.bfloat16)
    excess_two = placed(excess_home, states, jnp.bfloat16)
    rhs_two = placed(rhs_home, scenarios, jnp.float32)
    return lower_two, upper_two, excess_two, rhs_two


def solution(mesh):
    paired = mesh.shape["row"] == 4 and mesh.shape["tm"] % 2 == 0
    spec = P("tm", "row", None)

    def program(lower, upper, shift_diag, rhs):
        two_blocks = lower.shape[0] == 2 * mesh.shape["tm"]
        return jax.shard_map(
            shards_by_blocks if paired and two_blocks else shards_by_rows,
            mesh=mesh,
            in_specs=(spec, spec, P("tm", "row"), spec),
            out_specs=(spec,) * 4,
            check_vma=False,
        )(lower, upper, shift_diag, rhs)

    return program
```
